128 devices in a mesh: row: 8 (over z_hi, y), col: 16 (over z_lo, x, core).
Axes of the slice: x: 4, y: 4, z: 4 (z_hi: 2, z_lo: 2; z = z_hi * 2 + z_lo), core: 2. Of those that a mesh axis runs over, the one named last changes fastest.
Arguments:
- factors: bfloat16 [16384, 2048], P(('row', 'col')), may hold values from -6 to 6
- dressed: bfloat16 [16384, 2048], P(('col', 'row')), may hold values from -0.125 to 0.125
- amplitudes: float32 [640, 512, 512], P(('row', 'col')), may hold values from -2.4 to 2.4
- fock_vv: float32 [512, 512], replicated, as said below
- occ_energy: float32 [32], replicated, may hold values from -2 to -0.3
- pair_list: int32 [528, 2], replicated, may hold values from 0 to 31, as said below
- owner_map: int32 [528], replicated, may hold values from 0 to 127, as said below
Outputs:
- updated: float32 [640, 512, 512], P(('row', 'col'))
- pair_energy: float32 [640], P(('row', 'col'))
The draws below stay inside these ranges and needn't reach their ends.
Inputs may be any that keep to these rules, and one draw needn't show every extreme that they name: `pair_list`: every unordered pair of occupied orbitals appears exactly once, as i <= j. `owner_map`: each device owns 528 // 128 or 5 pairs, and some device owns exactly 5. `fock_vv`: Symmetric; its diagonal lies between 1 and 3.
All inputs are finite; a program needn't handle non-finite values.
Results may differ from the reference program's by a relative error of at most 0.0041.
Values may be sent and summed in bfloat16 or wider, within the bound.
No kernel may reach another device: no remote copies, remote signals or barrier semaphores. Data moves between devices by JAX's collectives and lax.ppermute only.
A program may use at most 128 MiB of HBM per device.

```python
import jax
import jax.numpy as jnp
from jax import lax

O = 32
V = 512
NAUX = 2048
NDEV = 128
NP = 16384
PAIRS = 528
CAP = 5


def draw_fock_vv(key, part):
    level = jax.random.uniform(jax.random.fold_in(key, 5), (V,), jnp.float32, 1.0, 3.0)
    noise = jax.random.normal(jax.random.fold_in(key, 6), (V, V), jnp.float32)
    spread = 0.5 / jnp.sqrt(jnp.float32(V))
    coupling = (noise + noise.T) * spread
    coupling = coupling * (1.0 - jnp.eye(V, dtype=jnp.float32))
    return coupling + jnp.diag(level)


def draw_pair_list(key, part):
    upper = jnp.triu(jnp.ones((O, O), jnp.int32))
    first_orbs, second_orbs = jnp.nonzero(upper, size=PAIRS)
    order = jax.random.permutation(jax.random.fold_in(key, 3), PAIRS)
    return jnp.stack([first_orbs[order], second_orbs[order]], axis=1).astype(jnp.int32)


def draw_owner_map(key, part):
    order = jax.random.permutation(jax.random.fold_in(key, 7), PAIRS)
    devices = jax.random.permutation(jax.random.fold_in(key, 11), NDEV)
    return devices[order % NDEV].astype(jnp.int32)


def block_scale(key, shape, cuts, low, top_value):
    level = 1.0
    for position, blocks in cuts:
        draws = jax.random.uniform(jax.random.fold_in(jax.random.fold_in(key, 6), position), (blocks,), jnp.float32, low / len(cuts), top_value / len(cuts))
        level = level * jnp.repeat(jnp.exp(draws), shape[position] // blocks).reshape((-1,) + (1,) * (len(shape) - 1 - position))
    return level


def normal_values(rng, extent, deviation, limit, pieces=(), held_as=jnp.bfloat16):
    values = jax.random.normal(rng, extent, jnp.float32) * deviation
    if len(pieces) > 0:
        values = block_scale(rng, extent, pieces, -0.22, 0.18) * values
    return jnp.clip(values, min=-limit, max=limit).astype(held_as)


def setup_inputs(seed: int = 0) -> dict:
    key_list = jax.random.split(jax.random.key(seed), 8)
    return {
        "factors": normal_values(key_list[0], (NP, NAUX), 1.0, 6.0, ((0, 128),)),
        "dressed": normal_values(key_list[1], (NP, NAUX), NAUX ** -0.5, 0.125, ((0, 128),)),
        "amplitudes": normal_values(key_list[2], (NDEV * CAP, V, V), 0.3, 2.4, ((0, 128),), jnp.float32),
        "fock_vv": draw_fock_vv(jax.random.fold_in(key_list[7], 71), 0),
        "occ_energy": jnp.clip(jax.random.uniform(key_list[4], (O,), jnp.float32, -2.0, -0.3), -2.0, -0.3),
        "pair_list": draw_pair_list(jax.random.fold_in(key_list[7], 71), 0),
        "owner_map": draw_owner_map(jax.random.fold_in(key_list[7], 71), 0),
    }


def reference(factors, dressed, amplitudes, fock_vv, occ_energy, pair_list, owner_map):
    highest = lax.Precision.HIGHEST
    orbital_level = jnp.diagonal(fock_vv)
    positions = jnp.arange(PAIRS, dtype=jnp.int32)
    same_owner = owner_map[:, None] == owner_map[None, :]
    earlier = positions[:, None] > positions[None, :]
    slot_index = jnp.sum((same_owner & earlier).astype(jnp.int32), axis=1)
    target = (owner_map * CAP + slot_index).astype(jnp.int32)

    def one_pair(inputs):
        pair_row, slot_at = inputs
        first_orb = pair_row[0]
        second_orb = pair_row[1]
        left_first = lax.dynamic_slice_in_dim(factors, (first_orb * V).astype(jnp.int32), V, 0)
        left_second = lax.dynamic_slice_in_dim(factors, (second_orb * V).astype(jnp.int32), V, 0)
        right_first = lax.dynamic_slice_in_dim(dressed, (first_orb * V).astype(jnp.int32), V, 0)
        right_second = lax.dynamic_slice_in_dim(dressed, (second_orb * V).astype(jnp.int32), V, 0)
        forward = jnp.dot(left_first, right_second.T, preferred_element_type=jnp.float32)
        backward = jnp.dot(left_second, right_first.T, preferred_element_type=jnp.float32)
        equal = first_orb == second_orb
        diagonal_part = 0.5 * (forward + forward.T)
        upper = jnp.where(equal, diagonal_part, forward).astype(jnp.bfloat16)
        lower = jnp.where(equal, diagonal_part, backward.T).astype(jnp.bfloat16)
        symmetric = (upper.astype(jnp.float32) + lower.astype(jnp.float32)).astype(jnp.bfloat16)
        source_part = symmetric.astype(jnp.float32)
        current = lax.dynamic_index_in_dim(amplitudes, slot_at, 0, keepdims=False)
        pair_shift = occ_energy[first_orb] + occ_energy[second_orb]
        residual = source_part + jnp.dot(fock_vv, current, precision=highest) + jnp.dot(current, fock_vv, precision=highest) - pair_shift * current
        denominator = orbital_level[:, None] + orbital_level[None, :] - pair_shift
        updated = current - residual / denominator
        energy = jnp.mean(source_part * updated)
        return updated, energy

    new_tiles, energies = lax.map(one_pair, (pair_list, target))
    updated = jnp.zeros((NDEV * CAP, V, V), jnp.float32).at[target].set(new_tiles)
    pair_energy = jnp.zeros((NDEV * CAP,), jnp.float32).at[target].set(energies)
    return updated, pair_energy
```

```python
import functools

import jax
import jax.numpy as jnp
from jax import lax
from jax.experimental import pallas as pl
from jax.experimental.pallas import tpu as pltpu
from jax.sharding import Mesh
from jax.sharding import PartitionSpec as P

AXES = ("zh", "y", "zl", "xh", "xl", "c")
SIZES = (2, 4, 2, 2, 2, 2)
DEVICES = 128
OCC = 32
VIRT = 512
AUX = 2048
ROWS = 32
COLS = 64
LANES = 128
LEFT = 4
RIGHT = 8
PIECE = 256
F32 = jnp.float32
BF16 = jnp.bfloat16


def tiles_kernel(first_tile, second_tile, spare_tile, flip_low, flip_high, *refs):
    left = refs[:LEFT]
    right = refs[LEFT : LEFT + RIGHT]
    out, left_buf, right_buf, grid_buf, left_sem, right_sem = refs[LEFT + RIGHT :]
    for n in range(LEFT):
        pltpu.make_async_copy(left[n], left_buf.at[pl.ds(n * PIECE, PIECE)], left_sem.at[n]).start()
    for n in range(RIGHT):
        pltpu.make_async_copy(right[n], right_buf.at[n], right_sem.at[n]).start()
    for n in range(LEFT):
        pltpu.make_async_copy(left[n], left_buf.at[pl.ds(n * PIECE, PIECE)], left_sem.at[n]).wait()
    for n in range(RIGHT):
        pltpu.make_async_copy(right[n], right_buf.at[n], right_sem.at[n]).wait()
        for m in range(LEFT):
            block = lax.dot_general(
                left_buf[m * PIECE : (m + 1) * PIECE, :],
                right_buf[n],
                (((1,), (1,)), ((), ())),
                preferred_element_type=F32,
            )
            for half in range(2):
                tile = block[:, half * LANES : (half + 1) * LANES]
                grid_buf[2 * n + half, m * 8 : (m + 1) * 8] = tile.reshape(8, ROWS, LANES)
    lane = lax.broadcasted_iota(jnp.int32, (ROWS, LANES), 1)

    def pack(slot, carry):
        low = grid_buf[second_tile[slot] // OCC, second_tile[slot] % OCC]
        high = grid_buf[first_tile[slot] // OCC, first_tile[slot] % OCC]
        spare = grid_buf[spare_tile[slot] // OCC, spare_tile[slot] % OCC]
        turned = pltpu.roll(spare, COLS, 1)
        turn = ((lane < COLS) & (flip_low[slot] > 0)) | ((lane >= COLS) & (flip_high[slot] > 0))
        plain = jnp.where(lane < COLS, low, high)
        out[slot] = jnp.where(turn, turned, plain).astype(BF16)
        return carry

    lax.fori_loop(0, out.shape[0], pack, 0, unroll=4)


def coupling_kernel(fock, amplitude, out):
    eye = lax.broadcasted_iota(jnp.int32, (VIRT, VIRT), 0) == lax.broadcasted_iota(jnp.int32, (VIRT, VIRT), 1)
    off = jnp.where(eye, 0.0, fock[...])
    current = amplitude[0]
    highest = lax.Precision.HIGHEST
    out[0] = jnp.dot(off, current, precision=highest, preferred_element_type=F32) + jnp.dot(
        current, off, precision=highest, preferred_element_type=F32
    )


def update_kernel(shift, live, fock, received, coupling, out, energy, forward, backward):
    slot = pl.program_id(0)
    lane = lax.broadcasted_iota(jnp.int32, (ROWS, LANES), 1)
    for zh in range(2):
        for xh in range(2):
            for quarter in range(4):
                start = quarter * 128 + (zh * 2 + xh) * ROWS
                for y in range(4):
                    at = ((zh * 4 + y) * 2 * 2 + xh) * 4 + quarter
                    even = received[at, 0].astype(F32)
                    odd = received[at + 8, 0].astype(F32)
                    forward[start : start + ROWS, y * LANES : (y + 1) * LANES] = jnp.where(
                        lane < COLS, pltpu.roll(even, COLS, 1), odd
                    )
                    backward[start : start + ROWS, y * LANES : (y + 1) * LANES] = jnp.where(
                        lane < COLS, even, pltpu.roll(odd, COLS, 1)
                    )
    source = (forward[...] + backward[...].T).astype(BF16).astype(F32)
    eye = lax.broadcasted_iota(jnp.int32, (VIRT, VIRT), 0) == lax.broadcasted_iota(jnp.int32, (VIRT, VIRT), 1)
    diagonal = jnp.where(eye, fock[...], 0.0)
    level_row = jnp.sum(diagonal, axis=0, keepdims=True)
    level_col = jnp.sum(diagonal, axis=1, keepdims=True)
    denominator = level_col + level_row - shift[slot]
    fresh = -(source + coupling[0]) / denominator
    fresh = jnp.where(live[slot] > 0, fresh, 0.0)
    out[0] = fresh
    total = jnp.sum(source * fresh) * (1.0 / (VIRT * VIRT))
    energy[...] = jnp.where(live[slot] > 0, jnp.full((1, 8, LANES), total, F32), 0.0)


def local(factors, dressed, amplitudes, fock_vv, occ_energy, pair_list, owner_map):
    capacity = amplitudes.shape[0]
    slots = DEVICES * capacity
    y_at = lax.axis_index("y")
    x_at = lax.axis_index("xh") * 2 + lax.axis_index("xl")
    c_at = lax.axis_index("c")

    right_send = jnp.concatenate([dressed, dressed], axis=0)
    right_own = lax.all_to_all(right_send, ("zh", "zl"), 0, 0, tiled=True)
    left_send = jnp.concatenate([factors[:64], factors[:64], factors[64:], factors[64:]], axis=0)
    left_own = lax.all_to_all(left_send, ("zh", "zl", "xh"), 0, 0, tiled=True)

    def ring(value, axis, step):
        return lax.ppermute(value, axis, [((n + step) % 4, n) for n in range(4)])

    left = [left_own] + [ring(left_own, "y", step) for step in (1, 3, 2)]
    right_mine = [right_own] + [ring(right_own, ("xh", "xl"), step) for step in (1, 3, 2)]
    right_other = [lax.ppermute(piece, "c", [(0, 1), (1, 0)]) for piece in right_mine]
    right = right_mine + right_other

    positions = jnp.arange(pair_list.shape[0], dtype=jnp.int32)
    same_owner = owner_map[:, None] == owner_map[None, :]
    earlier = positions[:, None] > positions[None, :]
    slot_index = jnp.sum((same_owner & earlier).astype(jnp.int32), axis=1)
    target = owner_map * capacity + slot_index
    slots_all = jnp.arange(slots, dtype=jnp.int32)
    filled = target[None, :] == slots_all[:, None]
    first_orb = jnp.sum(jnp.where(filled, pair_list[None, :, 0], 0), axis=1)
    second_orb = jnp.sum(jnp.where(filled, pair_list[None, :, 1], 0), axis=1)
    occupied = jnp.sum(filled.astype(jnp.int32), axis=1)

    def order(distance):
        return jnp.where(distance == 2, 3, jnp.where(distance == 3, 2, distance))

    def row_block(orb):
        piece = order((orb // 4 - y_at) % 4)
        return piece * 8 + orb // 16 * 4 + orb % 4

    def lane_group(orb):
        core = orb // 2 % 2
        piece = order((orb // 4 - x_at) % 4)
        return ((core != c_at).astype(jnp.int32) * 4 + piece) * 2 + orb % 2

    first_tile = lane_group(second_orb) * OCC + row_block(first_orb)
    second_tile = lane_group(first_orb) * OCC + row_block(second_orb)
    flip_high = (second_orb < 16).astype(jnp.int32)
    flip_low = (first_orb >= 16).astype(jnp.int32)
    spare_tile = jnp.where(flip_high > 0, first_tile, second_tile)

    smem = pl.BlockSpec(memory_space=pltpu.SMEM)
    hbm = pl.BlockSpec(memory_space=pl.ANY)
    vmem = pl.BlockSpec(memory_space=pltpu.VMEM)
    packed = pl.pallas_call(
        tiles_kernel,
        out_shape=jax.ShapeDtypeStruct((slots, ROWS, LANES), BF16),
        in_specs=[smem] * 5 + [hbm] * (LEFT + RIGHT),
        out_specs=vmem,
        scratch_shapes=[
            pltpu.VMEM((LEFT * PIECE, AUX), BF16),
            pltpu.VMEM((RIGHT, PIECE, AUX), BF16),
            pltpu.VMEM((2 * RIGHT, OCC, ROWS, LANES), F32),
            pltpu.SemaphoreType.DMA((LEFT,)),
            pltpu.SemaphoreType.DMA((RIGHT,)),
        ],
        compiler_params=pltpu.CompilerParams(vmem_limit_bytes=48 * 1024 * 1024),
        cost_estimate=pl.CostEstimate(
            flops=2 * 1024 * 2048 * AUX, bytes_accessed=18 * 1024 * 1024, transcendentals=0
        ),
        name="tiles",
    )(first_tile, second_tile, spare_tile, flip_low, flip_high, *left, *right)

    received = lax.all_to_all(packed, AXES, 0, 0, tiled=True)
    received = received.reshape(DEVICES, capacity, ROWS, LANES)

    coupling = pl.pallas_call(
        coupling_kernel,
        out_shape=jax.ShapeDtypeStruct((capacity, VIRT, VIRT), F32),
        grid=(capacity,),
        in_specs=[
            pl.BlockSpec((VIRT, VIRT), lambda s: (0, 0)),
            pl.BlockSpec((1, VIRT, VIRT), lambda s: (s, 0, 0)),
        ],
        out_specs=pl.BlockSpec((1, VIRT, VIRT), lambda s: (s, 0, 0)),
        compiler_params=pltpu.CompilerParams(vmem_limit_bytes=40 * 1024 * 1024),
        cost_estimate=pl.CostEstimate(
            flops=2 * 2 * 6 * capacity * VIRT**3, bytes_accessed=11 * 1024 * 1024, transcendentals=0
        ),
        name="coupling",
    )(fock_vv, amplitudes)

    own_index = (lax.axis_index("zh") * 4 + y_at) * 16 + lax.axis_index("zl") * 8 + x_at * 2 + c_at
    orbs = jnp.arange(OCC, dtype=jnp.int32)
    my_first = lax.dynamic_slice_in_dim(first_orb, own_index * capacity, capacity)
    my_second = lax.dynamic_slice_in_dim(second_orb, own_index * capacity, capacity)
    live = lax.dynamic_slice_in_dim(occupied, own_index * capacity, capacity)
    shift = jnp.sum(jnp.where(my_first[:, None] == orbs[None, :], occ_energy[None, :], 0.0), axis=1)
    shift = shift + jnp.sum(jnp.where(my_second[:, None] == orbs[None, :], occ_energy[None, :], 0.0), axis=1)

    updated, energy = pl.pallas_call(
        update_kernel,
        out_shape=(
            jax.ShapeDtypeStruct((capacity, VIRT, VIRT), F32),
            jax.ShapeDtypeStruct((capacity, 8, LANES), F32),
        ),
        grid=(capacity,),
        in_specs=[
            smem,
            smem,
            pl.BlockSpec((VIRT, VIRT), lambda s: (0, 0)),
            pl.BlockSpec((DEVICES, 1, ROWS, LANES), lambda s: (0, s, 0, 0)),
            pl.BlockSpec((1, VIRT, VIRT), lambda s: (s, 0, 0)),
        ],
        out_specs=(
            pl.BlockSpec((1, VIRT, VIRT), lambda s: (s, 0, 0)),
            pl.BlockSpec((1, 8, LANES), lambda s: (s, 0, 0)),
        ),
        scratch_shapes=[pltpu.VMEM((VIRT, VIRT), F32), pltpu.VMEM((VIRT, VIRT), F32)],
        compiler_params=pltpu.CompilerParams(vmem_limit_bytes=40 * 1024 * 1024),
        name="update",
    )(shift, live, fock_vv, received, coupling)
    return updated, energy[:, 0, 0]


def solution(mesh):
    fine = Mesh(mesh.devices.reshape(SIZES), AXES)
    return jax.shard_map(
        local,
        mesh=fine,
        in_specs=(
            P(AXES, None),
            P(("zl", "xh", "xl", "c", "zh", "y"), None),
            P(AXES, None, None),
            P(),
            P(),
            P(),
            P(),
        ),
        out_specs=(P(AXES, None, None), P(AXES)),
        check_vma=False,
    )
```

```python
import functools

import jax
import jax.numpy as jnp
from jax import lax
from jax.experimental import pallas as pl
from jax.experimental.pallas import tpu as pltpu
from jax.sharding import Mesh
from jax.sharding import PartitionSpec as P

AXES = ("zh", "y", "zl", "xh", "xl", "c")
SIZES = (2, 4, 2, 2, 2, 2)
DEVICES = 128
OCC = 32
VIRT = 512
AUX = 2048
ROWS = 32
COLS = 64
LANES = 128
PIECE = 256
EARLY_GROUPS = 13
CHUNKS = 5
MIB = 1024 * 1024
F32 = jnp.float32
BF16 = jnp.bfloat16


def product(left, right):
    return lax.dot_general(left, right, (((1,), (1,)), ((), ())), preferred_element_type=F32).astype(BF16)


def store_tiles(buf, group, block, value):
    for half in range(value.shape[1] // LANES):
        part = value[:, half * LANES : (half + 1) * LANES]
        buf[group + half, pl.ds(block, value.shape[0] // ROWS)] = part.reshape(-1, ROWS, LANES)


def fill(refs, buf, sem):
    copies = []
    start = 0
    for n, ref in enumerate(refs):
        copies.append(pltpu.make_async_copy(ref, buf.at[pl.ds(start, ref.shape[0])], sem.at[n]))
        start += ref.shape[0]
    for copy in copies:
        copy.start()
    return copies


def early_kernel(*refs):
    left = refs[:3]
    right = refs[3:17]
    out, left_buf, right_buf, left_sem, right_sem = refs[17:]
    left_copies = fill(left, left_buf, left_sem)
    right_copies = fill(right, right_buf, right_sem)
    for copy in left_copies:
        copy.wait()
    done = 0
    for start, size, count in ((0, 512, 8), (512, 384, 2), (896, 384, 2), (1280, 384, 2)):
        for copy in right_copies[done : done + count]:
            copy.wait()
        done += count
        for m in range(3):
            value = product(left_buf[m * PIECE : (m + 1) * PIECE, :], right_buf[start : start + size, :])
            store_tiles(out, start // LANES, m * 8, value)


def late_kernel(low_tile, high_tile, low_from, high_from, early, *refs):
    left = refs[:4]
    right = refs[4:20]
    out, left_buf, right_buf, grid_buf, out_buf, early_sem, left_sem, right_sem, out_sem = refs[20:]
    early_copy = pltpu.make_async_copy(
        early, grid_buf.at[pl.ds(0, EARLY_GROUPS), pl.ds(0, 24)], early_sem.at[0]
    )
    left_copies = fill(left, left_buf, left_sem)
    right_copies = fill(right, right_buf, right_sem)
    early_copy.start()
    left_copies[0].wait()
    done = 0
    for start, size, count in ((0, 384, 2), (384, 512, 8), (896, 384, 2), (1280, 384, 2), (1664, 384, 2)):
        for copy in right_copies[done : done + count]:
            copy.wait()
        done += count
        group = EARLY_GROUPS if start == 0 else (start - 384) // LANES
        store_tiles(grid_buf, group, 24, product(left_buf[0:PIECE, :], right_buf[start : start + size, :]))
    for m in range(3):
        left_copies[m + 1].wait()
        value = product(left_buf[(m + 1) * PIECE : (m + 2) * PIECE, :], right_buf[0:384, :])
        store_tiles(grid_buf, EARLY_GROUPS, m * 8, value)
    early_copy.wait()
    lane = lax.broadcasted_iota(jnp.int32, (ROWS, LANES), 1)
    lower = lane < COLS

    def pack(slot, carry):
        low = grid_buf[low_tile[slot] // OCC, low_tile[slot] % OCC].astype(F32)
        high = grid_buf[high_tile[slot] // OCC, high_tile[slot] % OCC].astype(F32)
        plain = jnp.where(lower, low, high)
        turned = pltpu.roll(jnp.where(lower, high, low), COLS, 1)
        turn = jnp.where(lower, low_from[slot], high_from[slot])
        out_buf[slot] = jnp.where(turn > 0, turned, plain).astype(BF16)
        return carry

    copies = []
    for chunk in range(CHUNKS):
        size = out.shape[0] // CHUNKS
        lax.fori_loop(chunk * size, (chunk + 1) * size, pack, 0, unroll=8)
        span = pl.ds(chunk * size, size)
        copies.append(pltpu.make_async_copy(out_buf.at[span], out.at[span], out_sem.at[chunk]))
        copies[-1].start()
    for copy in copies:
        copy.wait()


def coupling_kernel(fock, amplitude, out):
    eye = lax.broadcasted_iota(jnp.int32, (VIRT, VIRT), 0) == lax.broadcasted_iota(jnp.int32, (VIRT, VIRT), 1)
    off = jnp.where(eye, 0.0, fock[...])
    current = amplitude[0]
    highest = lax.Precision.HIGHEST
    out[0] = jnp.dot(off, current, precision=highest, preferred_element_type=F32) + jnp.dot(
        current, off, precision=highest, preferred_element_type=F32
    )


def update_kernel(shift, live, fock, received, coupling, out, energy, forward, backward):
    slot = pl.program_id(0)
    lane = lax.broadcasted_iota(jnp.int32, (ROWS, LANES), 1)
    for zh in range(2):
        for xh in range(2):
            for quarter in range(4):
                start = quarter * 128 + (zh * 2 + xh) * ROWS
                for y in range(4):
                    at = ((zh * 4 + y) * 2 * 2 + xh) * 4 + quarter
                    even = received[at, 0].astype(F32)
                    odd = received[at + 8, 0].astype(F32)
                    forward[start : start + ROWS, y * LANES : (y + 1) * LANES] = jnp.where(
                        lane < COLS, pltpu.roll(even, COLS, 1), odd
                    )
                    backward[start : start + ROWS, y * LANES : (y + 1) * LANES] = jnp.where(
                        lane < COLS, even, pltpu.roll(odd, COLS, 1)
                    )
    source = (forward[...] + backward[...].T).astype(BF16).astype(F32)
    eye = lax.broadcasted_iota(jnp.int32, (VIRT, VIRT), 0) == lax.broadcasted_iota(jnp.int32, (VIRT, VIRT), 1)
    diagonal = jnp.where(eye, fock[...], 0.0)
    level_row = jnp.sum(diagonal, axis=0, keepdims=True)
    level_col = jnp.sum(diagonal, axis=1, keepdims=True)
    denominator = level_col + level_row - shift[slot]
    fresh = -(source + coupling[0]) / denominator
    fresh = jnp.where(live[slot] > 0, fresh, 0.0)
    out[0] = fresh
    total = jnp.sum(source * fresh) * (1.0 / (VIRT * VIRT))
    energy[...] = jnp.where(live[slot] > 0, jnp.full((1, 8, LANES), total, F32), 0.0)


def local(factors, dressed, amplitudes, fock_vv, occ_energy, pair_list, owner_map):
    capacity = amplitudes.shape[0]
    slots = DEVICES * capacity
    y_at = lax.axis_index("y")
    x_at = lax.axis_index("xh") * 2 + lax.axis_index("xl")
    c_at = lax.axis_index("c")
    zh_at = lax.axis_index("zh")
    zl_at = lax.axis_index("zl")

    def ring(value, axis, step):
        return lax.ppermute(value, axis, [((n + step) % 4, n) for n in range(4)])

    def across(value, flip):
        return lax.ppermute(value, ("zh", "zl"), [(n, n ^ flip) for n in range(4)])

    def other_core(value):
        return lax.ppermute(value, "c", [(0, 1), (1, 0)])

    left_send = jnp.concatenate([factors[:64], factors[:64], factors[64:], factors[64:]], axis=0)
    left_own = lax.all_to_all(left_send, ("zh", "zl", "xh"), 0, 0, tiled=True)
    kept = lax.dynamic_slice_in_dim(dressed, zl_at * COLS, COLS)
    given = lax.dynamic_slice_in_dim(dressed, (1 - zl_at) * COLS, COLS)
    rest = jnp.concatenate([across(given, 1), across(kept, 2), across(given, 3)], axis=0)
    steps = (1, 3, 2)
    axis = ("xh", "xl")
    near = [kept] + [ring(kept, axis, step) for step in steps]
    far = [rest] + [ring(rest, axis, step) for step in steps]
    left = [left_own] + [ring(left_own, "y", step) for step in steps]
    near = near + [other_core(piece) for piece in near]
    far_other = [other_core(piece) for piece in far]
    far_early = far[:3] + far_other[:3]
    far_late = [far[3], far_other[3]]

    positions = jnp.arange(pair_list.shape[0], dtype=jnp.int32)
    same_owner = owner_map[:, None] == owner_map[None, :]
    earlier = positions[:, None] > positions[None, :]
    slot_index = jnp.sum((same_owner & earlier).astype(jnp.int32), axis=1)
    target = owner_map * capacity + slot_index
    slots_all = jnp.arange(slots, dtype=jnp.int32)
    filled = target[None, :] == slots_all[:, None]
    first_orb = jnp.sum(jnp.where(filled, pair_list[None, :, 0], 0), axis=1)
    second_orb = jnp.sum(jnp.where(filled, pair_list[None, :, 1], 0), axis=1)
    occupied = jnp.sum(filled.astype(jnp.int32), axis=1)

    def order(distance):
        return jnp.where(distance == 2, 3, jnp.where(distance == 3, 2, distance))

    def row_block(orb):
        piece = order((orb // 4 - y_at) % 4)
        return piece * 8 + orb // 16 * 4 + orb % 4

    def column(orb):
        core = (orb // 2 % 2 != c_at).astype(jnp.int32)
        piece = order((orb // 4 - x_at) % 4)
        level = (orb % 2 != zh_at).astype(jnp.int32) * 2 + (orb // 16 != zl_at).astype(jnp.int32)
        apart = jnp.where(piece == 3, 18 + core * 3, (core * 3 + piece) * 3) + 7 + level
        return jnp.where(level == 0, core * 4 + piece, apart)

    first_column = column(first_orb)
    second_column = column(second_orb)
    high_tile = second_column // 2 * OCC + row_block(first_orb)
    low_tile = first_column // 2 * OCC + row_block(second_orb)
    high_from = 1 - second_column % 2
    low_from = first_column % 2

    smem = pl.BlockSpec(memory_space=pltpu.SMEM)
    hbm = pl.BlockSpec(memory_space=pl.ANY)
    vmem = pl.BlockSpec(memory_space=pltpu.VMEM)
    early = pl.pallas_call(
        early_kernel,
        out_shape=jax.ShapeDtypeStruct((EARLY_GROUPS, 24, ROWS, LANES), BF16),
        in_specs=[hbm] * 17,
        out_specs=vmem,
        scratch_shapes=[
            pltpu.VMEM((3 * PIECE, AUX), BF16),
            pltpu.VMEM((EARLY_GROUPS * LANES, AUX), BF16),
            pltpu.SemaphoreType.DMA((3,)),
            pltpu.SemaphoreType.DMA((14,)),
        ],
        compiler_params=pltpu.CompilerParams(vmem_limit_bytes=40 * MIB),
        cost_estimate=pl.CostEstimate(
            flops=2 * 768 * 1664 * AUX, bytes_accessed=13 * MIB, transcendentals=0
        ),
        name="early",
    )(*left[:3], *near, *far_early)
    packed = pl.pallas_call(
        late_kernel,
        out_shape=jax.ShapeDtypeStruct((slots, ROWS, LANES), BF16),
        in_specs=[smem] * 4 + [hbm] * 21,
        out_specs=hbm,
        scratch_shapes=[
            pltpu.VMEM((4 * PIECE, AUX), BF16),
            pltpu.VMEM((2048, AUX), BF16),
            pltpu.VMEM((16, OCC, ROWS, LANES), BF16),
            pltpu.VMEM((slots, ROWS, LANES), BF16),
            pltpu.SemaphoreType.DMA((1,)),
            pltpu.SemaphoreType.DMA((4,)),
            pltpu.SemaphoreType.DMA((16,)),
            pltpu.SemaphoreType.DMA((CHUNKS,)),
        ],
        compiler_params=pltpu.CompilerParams(vmem_limit_bytes=48 * MIB),
        cost_estimate=pl.CostEstimate(
            flops=2 * (256 * 2048 + 768 * 384) * AUX, bytes_accessed=18 * MIB, transcendentals=0
        ),
        name="late",
    )(low_tile, high_tile, low_from, high_from, early, left[3], *left[:3], *far_late, *near, *far_early)

    received = lax.all_to_all(packed, AXES, 0, 0, tiled=True)
    received = received.reshape(DEVICES, capacity, ROWS, LANES)

    coupling = pl.pallas_call(
        coupling_kernel,
        out_shape=jax.ShapeDtypeStruct((capacity, VIRT, VIRT), F32),
        grid=(capacity,),
        in_specs=[
            pl.BlockSpec((VIRT, VIRT), lambda s: (0, 0)),
            pl.BlockSpec((1, VIRT, VIRT), lambda s: (s, 0, 0)),
        ],
        out_specs=pl.BlockSpec((1, VIRT, VIRT), lambda s: (s, 0, 0)),
        compiler_params=pltpu.CompilerParams(vmem_limit_bytes=56 * MIB),
        cost_estimate=pl.CostEstimate(
            flops=2 * 2 * 6 * capacity * VIRT**3, bytes_accessed=11 * MIB, transcendentals=0
        ),
        name="coupling",
    )(fock_vv, amplitudes)

    own_index = (lax.axis_index("zh") * 4 + y_at) * 16 + lax.axis_index("zl") * 8 + x_at * 2 + c_at
    orbs = jnp.arange(OCC, dtype=jnp.int32)
    my_first = lax.dynamic_slice_in_dim(first_orb, own_index * capacity, capacity)
    my_second = lax.dynamic_slice_in_dim(second_orb, own_index * capacity, capacity)
    live = lax.dynamic_slice_in_dim(occupied, own_index * capacity, capacity)
    shift = jnp.sum(jnp.where(my_first[:, None] == orbs[None, :], occ_energy[None, :], 0.0), axis=1)
    shift = shift + jnp.sum(jnp.where(my_second[:, None] == orbs[None, :], occ_energy[None, :], 0.0), axis=1)

    updated, energy = pl.pallas_call(
        update_kernel,
        out_shape=(
            jax.ShapeDtypeStruct((capacity, VIRT, VIRT), F32),
            jax.ShapeDtypeStruct((capacity, 8, LANES), F32),
        ),
        grid=(capacity,),
        in_specs=[
            smem,
            smem,
            pl.BlockSpec((VIRT, VIRT), lambda s: (0, 0)),
            pl.BlockSpec((DEVICES, 1, ROWS, LANES), lambda s: (0, s, 0, 0)),
            pl.BlockSpec((1, VIRT, VIRT), lambda s: (s, 0, 0)),
        ],
        out_specs=(
            pl.BlockSpec((1, VIRT, VIRT), lambda s: (s, 0, 0)),
            pl.BlockSpec((1, 8, LANES), lambda s: (s, 0, 0)),
        ),
        scratch_shapes=[pltpu.VMEM((VIRT, VIRT), F32), pltpu.VMEM((VIRT, VIRT), F32)],
        compiler_params=pltpu.CompilerParams(vmem_limit_bytes=56 * MIB),
        name="update",
    )(shift, live, fock_vv, received, coupling)
    return updated, energy[:, 0, 0]


def solution(mesh):
    fine = Mesh(mesh.devices.reshape(SIZES), AXES)
    return jax.shard_map(
        local,
        mesh=fine,
        in_specs=(
            P(AXES, None),
            P(("zl", "xh", "xl", "c", "zh", "y"), None),
            P(AXES, None, None),
            P(),
            P(),
            P(),
            P(),
        ),
        out_specs=(P(AXES, None, None), P(AXES)),
        check_vma=False,
    )
```

```python
import functools

import jax
import jax.numpy as jnp
from jax import lax
from jax.experimental import pallas as pl
from jax.experimental.pallas import tpu as pltpu
from jax.sharding import Mesh
from jax.sharding import PartitionSpec as P

AXES = ("zh", "y", "zl", "xh", "xl", "c")
SIZES = (2, 4, 2, 2, 2, 2)
DEVICES = 128
OCC = 32
VIRT = 512
AUX = 2048
ROWS = 32
COLS = 64
LANES = 128
PIECE = 128
LEFT = 8
EARLY = 14
RIGHT = 16
CHUNKS = 5
MIB = 1024 * 1024
F32 = jnp.float32
BF16 = jnp.bfloat16


def product(left, right):
    return lax.dot_general(left, right, (((1,), (1,)), ((), ())), preferred_element_type=F32)


def store_tiles(buf, group, value):
    for half in range(value.shape[1] // LANES):
        part = value[:, half * LANES : (half + 1) * LANES]
        buf[0, group + half] = part.astype(BF16).reshape(-1, ROWS, LANES)
        buf[1, group + half] = pltpu.roll(part, COLS, 1).astype(BF16).reshape(-1, ROWS, LANES)


def fill(refs, buf, sem):
    copies = []
    for n, ref in enumerate(refs):
        copies.append(pltpu.make_async_copy(ref, buf.at[pl.ds(n * PIECE, PIECE)], sem.at[n]))
    return copies


def early_kernel(*refs):
    left = refs[:LEFT]
    right = refs[LEFT : LEFT + EARLY]
    out, left_buf, right_buf, left_sem, right_sem = refs[LEFT + EARLY :]
    left_copies = fill(left, left_buf, left_sem)
    right_copies = fill(right, right_buf, right_sem)
    for copy in right_copies[:2] + left_copies + right_copies[2:]:
        copy.start()
    for copy in left_copies:
        copy.wait()
    for group in range(0, EARLY, 2):
        right_copies[group].wait()
        right_copies[group + 1].wait()
        store_tiles(out, group, product(left_buf[...], right_buf[group * PIECE : (group + 2) * PIECE, :]))


def late_kernel(low_tile, high_tile, early, *refs):
    left = refs[:LEFT]
    right = refs[LEFT : LEFT + 2]
    out, left_buf, right_buf, grid_buf, out_buf, early_sem, left_sem, right_sem, out_sem = refs[LEFT + 2 :]
    early_copy = pltpu.make_async_copy(early, grid_buf.at[:, pl.ds(0, EARLY)], early_sem.at[0])
    left_copies = fill(left, left_buf, left_sem)
    right_copies = fill(right, right_buf, right_sem)
    for copy in right_copies + left_copies:
        copy.start()
    early_copy.start()
    for copy in right_copies + left_copies:
        copy.wait()
    store_tiles(grid_buf, EARLY, product(left_buf[...], right_buf[...]))
    early_copy.wait()
    lower = lax.broadcasted_iota(jnp.int32, (ROWS, LANES), 1) < COLS

    def tile(index):
        return grid_buf[index // (RIGHT * OCC), index // OCC % RIGHT, index % OCC]

    def pack(slot, carry):
        out_buf[slot] = jnp.where(lower, tile(low_tile[slot]), tile(high_tile[slot]))
        return carry

    copies = []
    for chunk in range(CHUNKS):
        size = out.shape[0] // CHUNKS
        lax.fori_loop(chunk * size, (chunk + 1) * size, pack, 0, unroll=8)
        span = pl.ds(chunk * size, size)
        copies.append(pltpu.make_async_copy(out_buf.at[span], out.at[span], out_sem.at[chunk]))
        copies[-1].start()
    for copy in copies:
        copy.wait()


def coupling_kernel(fock, amplitude, out):
    eye = lax.broadcasted_iota(jnp.int32, (VIRT, VIRT), 0) == lax.broadcasted_iota(jnp.int32, (VIRT, VIRT), 1)
    off = jnp.where(eye, 0.0, fock[...])
    current = amplitude[0]
    highest = lax.Precision.HIGHEST
    out[0] = jnp.dot(off, current, precision=highest, preferred_element_type=F32) + jnp.dot(
        current, off, precision=highest, preferred_element_type=F32
    )


def update_kernel(shift, live, fock, received, coupling, out, energy, forward, backward):
    slot = pl.program_id(0)
    lane = lax.broadcasted_iota(jnp.int32, (ROWS, LANES), 1)
    for zh in range(2):
        for xh in range(2):
            for quarter in range(4):
                start = quarter * 128 + (zh * 2 + xh) * ROWS
                for y in range(4):
                    at = ((zh * 4 + y) * 2 * 2 + xh) * 4 + quarter
                    even = received[at, 0].astype(F32)
                    odd = received[at + 8, 0].astype(F32)
                    forward[start : start + ROWS, y * LANES : (y + 1) * LANES] = jnp.where(
                        lane < COLS, pltpu.roll(even, COLS, 1), odd
                    )
                    backward[start : start + ROWS, y * LANES : (y + 1) * LANES] = jnp.where(
                        lane < COLS, even, pltpu.roll(odd, COLS, 1)
                    )
    source = (forward[...] + backward[...].T).astype(BF16).astype(F32)
    eye = lax.broadcasted_iota(jnp.int32, (VIRT, VIRT), 0) == lax.broadcasted_iota(jnp.int32, (VIRT, VIRT), 1)
    diagonal = jnp.where(eye, fock[...], 0.0)
    level_row = jnp.sum(diagonal, axis=0, keepdims=True)
    level_col = jnp.sum(diagonal, axis=1, keepdims=True)
    denominator = level_col + level_row - shift[slot]
    fresh = -(source + coupling[0]) / denominator
    fresh = jnp.where(live[slot] > 0, fresh, 0.0)
    out[0] = fresh
    total = jnp.sum(source * fresh) * (1.0 / (VIRT * VIRT))
    energy[...] = jnp.where(live[slot] > 0, jnp.full((1, 8, LANES), total, F32), 0.0)


def local(factors, dressed, amplitudes, fock_vv, occ_energy, pair_list, owner_map):
    capacity = amplitudes.shape[0]
    slots = DEVICES * capacity
    y_at = lax.axis_index("y")
    x_at = lax.axis_index("xh") * 2 + lax.axis_index("xl")
    c_at = lax.axis_index("c")
    zh_at = lax.axis_index("zh")
    zl_at = lax.axis_index("zl")

    xh_at = lax.axis_index("xh")

    def ring(value, axis, step):
        return lax.ppermute(value, axis, [((n + step) % 4, n) for n in range(4)])

    def rings(value, axis, step):
        plus = ring(value, axis, 1)
        minus = ring(value, axis, 3)
        return [value, plus, minus, ring(plus if step == 1 else minus, axis, step)]

    def swap(value, axis):
        return lax.ppermute(value, axis, [(0, 1), (1, 0)])

    slab = zh_at * 2 + xh_at
    parts = [lax.dynamic_slice_in_dim(factors, slab * ROWS, ROWS)]
    for flip in (1, 2, 3):
        sent = lax.dynamic_slice_in_dim(factors, (slab ^ flip) * ROWS, ROWS)
        parts.append(lax.ppermute(sent, ("zh", "xh"), [(n, n ^ flip) for n in range(4)]))
    left_one = jnp.concatenate(parts, axis=0)
    left_two = swap(left_one, "zl")
    kept = lax.dynamic_slice_in_dim(dressed, zl_at * COLS, COLS)
    given = lax.dynamic_slice_in_dim(dressed, (1 - zl_at) * COLS, COLS)
    right_one = jnp.concatenate([kept, swap(given, "zl")], axis=0)
    right_two = swap(right_one, "zh")
    left = rings(left_one, "y", 1) + rings(left_two, "y", 3)
    right = []
    for piece in rings(right_one, ("xh", "xl"), 1) + rings(right_two, ("xh", "xl"), 3):
        right += [piece, swap(piece, "c")]

    positions = jnp.arange(pair_list.shape[0], dtype=jnp.int32)
    same_owner = owner_map[:, None] == owner_map[None, :]
    earlier = positions[:, None] > positions[None, :]
    slot_index = jnp.sum((same_owner & earlier).astype(jnp.int32), axis=1)
    target = owner_map * capacity + slot_index
    slots_all = jnp.arange(slots, dtype=jnp.int32)
    filled = target[None, :] == slots_all[:, None]
    first_orb = jnp.sum(jnp.where(filled, pair_list[None, :, 0], 0), axis=1)
    second_orb = jnp.sum(jnp.where(filled, pair_list[None, :, 1], 0), axis=1)
    occupied = jnp.sum(filled.astype(jnp.int32), axis=1)

    def order(distance):
        return jnp.where(distance == 2, 3, jnp.where(distance == 3, 2, distance))

    def row_block(orb):
        level = (orb // 2 % 2 != zl_at).astype(jnp.int32)
        flip = (orb // 16 != zh_at).astype(jnp.int32) * 2 + (orb % 2 != xh_at).astype(jnp.int32)
        return (level * 4 + order((orb // 4 - y_at) % 4)) * 4 + flip

    def group(orb):
        core = (orb // 2 % 2 != c_at).astype(jnp.int32)
        level = (orb % 2 != zh_at).astype(jnp.int32)
        return level * 8 + order((orb // 4 - x_at) % 4) * 2 + core

    def half(orb):
        return (orb // 16 != zl_at).astype(jnp.int32)

    high_tile = ((1 - half(second_orb)) * RIGHT + group(second_orb)) * OCC + row_block(first_orb)
    low_tile = (half(first_orb) * RIGHT + group(first_orb)) * OCC + row_block(second_orb)

    smem = pl.BlockSpec(memory_space=pltpu.SMEM)
    hbm = pl.BlockSpec(memory_space=pl.ANY)
    vmem = pl.BlockSpec(memory_space=pltpu.VMEM)
    early = pl.pallas_call(
        early_kernel,
        out_shape=jax.ShapeDtypeStruct((2, EARLY, OCC, ROWS, LANES), BF16),
        in_specs=[hbm] * (LEFT + EARLY),
        out_specs=vmem,
        scratch_shapes=[
            pltpu.VMEM((LEFT * PIECE, AUX), BF16),
            pltpu.VMEM((EARLY * PIECE, AUX), BF16),
            pltpu.SemaphoreType.DMA((LEFT,)),
            pltpu.SemaphoreType.DMA((EARLY,)),
        ],
        compiler_params=pltpu.CompilerParams(vmem_limit_bytes=48 * MIB),
        cost_estimate=pl.CostEstimate(
            flops=2 * 1024 * EARLY * PIECE * AUX, bytes_accessed=18 * MIB, transcendentals=0
        ),
        name="early",
    )(*left, *right[:EARLY])
    packed = pl.pallas_call(
        late_kernel,
        out_shape=jax.ShapeDtypeStruct((slots, ROWS, LANES), BF16),
        in_specs=[smem] * 2 + [hbm] * (LEFT + 3),
        out_specs=hbm,
        scratch_shapes=[
            pltpu.VMEM((LEFT * PIECE, AUX), BF16),
            pltpu.VMEM((2 * PIECE, AUX), BF16),
            pltpu.VMEM((2, RIGHT, OCC, ROWS, LANES), BF16),
            pltpu.VMEM((slots, ROWS, LANES), BF16),
            pltpu.SemaphoreType.DMA((1,)),
            pltpu.SemaphoreType.DMA((LEFT,)),
            pltpu.SemaphoreType.DMA((2,)),
            pltpu.SemaphoreType.DMA((CHUNKS,)),
        ],
        compiler_params=pltpu.CompilerParams(vmem_limit_bytes=48 * MIB),
        cost_estimate=pl.CostEstimate(
            flops=2 * 1024 * 256 * AUX, bytes_accessed=18 * MIB, transcendentals=0
        ),
        name="late",
    )(low_tile, high_tile, early, *left, *right[EARLY:])

    received = lax.all_to_all(packed, AXES, 0, 0, tiled=True)
    received = received.reshape(DEVICES, capacity, ROWS, LANES)

    coupling = pl.pallas_call(
        coupling_kernel,
        out_shape=jax.ShapeDtypeStruct((capacity, VIRT, VIRT), F32),
        grid=(capacity,),
        in_specs=[
            pl.BlockSpec((VIRT, VIRT), lambda s: (0, 0)),
            pl.BlockSpec((1, VIRT, VIRT), lambda s: (s, 0, 0)),
        ],
        out_specs=pl.BlockSpec((1, VIRT, VIRT), lambda s: (s, 0, 0)),
        compiler_params=pltpu.CompilerParams(vmem_limit_bytes=56 * MIB),
        cost_estimate=pl.CostEstimate(
            flops=2 * 2 * 6 * capacity * VIRT**3, bytes_accessed=11 * MIB, transcendentals=0
        ),
        name="coupling",
    )(fock_vv, amplitudes)

    own_index = (lax.axis_index("zh") * 4 + y_at) * 16 + lax.axis_index("zl") * 8 + x_at * 2 + c_at
    orbs = jnp.arange(OCC, dtype=jnp.int32)
    my_first = lax.dynamic_slice_in_dim(first_orb, own_index * capacity, capacity)
    my_second = lax.dynamic_slice_in_dim(second_orb, own_index * capacity, capacity)
    live = lax.dynamic_slice_in_dim(occupied, own_index * capacity, capacity)
    shift = jnp.sum(jnp.where(my_first[:, None] == orbs[None, :], occ_energy[None, :], 0.0), axis=1)
    shift = shift + jnp.sum(jnp.where(my_second[:, None] == orbs[None, :], occ_energy[None, :], 0.0), axis=1)

    updated, energy = pl.pallas_call(
        update_kernel,
        out_shape=(
            jax.ShapeDtypeStruct((capacity, VIRT, VIRT), F32),
            jax.ShapeDtypeStruct((capacity, 8, LANES), F32),
        ),
        grid=(capacity,),
        in_specs=[
            smem,
            smem,
            pl.BlockSpec((VIRT, VIRT), lambda s: (0, 0)),
            pl.BlockSpec((DEVICES, 1, ROWS, LANES), lambda s: (0, s, 0, 0)),
            pl.BlockSpec((1, VIRT, VIRT), lambda s: (s, 0, 0)),
        ],
        out_specs=(
            pl.BlockSpec((1, VIRT, VIRT), lambda s: (s, 0, 0)),
            pl.BlockSpec((1, 8, LANES), lambda s: (s, 0, 0)),
        ),
        scratch_shapes=[pltpu.VMEM((VIRT, VIRT), F32), pltpu.VMEM((VIRT, VIRT), F32)],
        compiler_params=pltpu.CompilerParams(vmem_limit_bytes=56 * MIB),
        name="update",
    )(shift, live, fock_vv, received, coupling)
    return updated, energy[:, 0, 0]


def solution(mesh):
    fine = Mesh(mesh.devices.reshape(SIZES), AXES)
    return jax.shard_map(
        local,
        mesh=fine,
        in_specs=(
            P(AXES, None),
            P(("zl", "xh", "xl", "c", "zh", "y"), None),
            P(AXES, None, None),
            P(),
            P(),
            P(),
            P(),
        ),
        out_specs=(P(AXES, None, None), P(AXES)),
        check_vma=False,
    )
```
